32 devices in a mesh: fsdp: 4 (over z), replica: 2 (over x), tensor: 4 (over y, core).
Axes of the slice: x: 2, y: 2, z: 4, core: 2. Of those that a mesh axis runs over, the one named last changes fastest.
Arguments:
- tokens: bfloat16 [1024, 8192], P(('fsdp', 'replica')), may hold values from -6 to 6
- weight_codes: bfloat16 [8192, 14336], P('fsdp', 'tensor'), may hold values from -127 to 127, as said below
- scales: float32 [64, 14336], P('fsdp', 'tensor'), may hold values from 3e-05 to 0.0003
- cotangent: bfloat16 [1024, 14336], P(('fsdp', 'replica'), 'tensor'), may hold values from -6 to 6
- sign_bits: int32 [14336], P('tensor'), may hold values from 0 to 1
Outputs:
- activation: bfloat16 [1024, 14336], P(('fsdp', 'replica'), 'tensor')
- input_grad: bfloat16 [1024, 8192], P(('fsdp', 'replica'), 'tensor')
- grad_codes: float32 [8192, 14336], P(('fsdp', 'replica'), 'tensor')
The draws below stay inside these ranges and needn't reach their ends.
Inputs may be any that keep to these rules, and one draw needn't show every extreme that they name: `weight_codes`: integer values, held exactly.
All inputs are finite; a program needn't handle non-finite values.
Results may differ from the reference program's by a relative error of at most 0.015.
Values may be sent and summed in bfloat16 or wider, within the bound.
A program may use at most 128 MiB of HBM per device.

```python
import math
import jax
import jax.numpy as jnp
from jax import lax

D = 8192
FF = 14336
QB = 128
HB = 128
TOKENS = 1024
N_FSDP = 4
N_TENSOR = 4


def draw_weight_codes(key, part):
    return jax.random.randint(key, (D, FF), -127, 128).astype(jnp.float32).astype(jnp.bfloat16)


def plant(result, stream_key, least, top_value):
    longest = result.shape.index(max(result.shape))
    spots = []
    for shift in (0, 1):
        where = [jax.random.randint(jax.random.fold_in(stream_key, axis), (), 0, length) for axis, length in enumerate(result.shape)]
        where[longest] = (where[longest] + shift) % result.shape[longest]
        spots.append(tuple(where))
    return result.at[spots[0]].set(least).at[spots[1]].set(top_value)


def block_levels(own_key, dims, shards, low, top_value):
    def one(dim, shards_of):
        heights = jax.random.uniform(jax.random.fold_in(jax.random.fold_in(own_key, 6), dim), (shards_of,), jnp.float32, low / len(shards), top_value / len(shards))
        return jnp.repeat(jnp.exp(heights), dims[dim] // shards_of).reshape((-1,) + (1,) * (len(dims) - dim - 1))

    level = one(*shards[0])
    for cut in shards[1:]:
        level = level * one(*cut)
    return level


def scatter_about(key, dims, scale, limit, split=(), kind=jnp.bfloat16):
    values = jax.random.normal(key, dims, jnp.float32) * scale
    if len(split) > 0:
        values = block_levels(key, dims, split, -0.22, 0.18) * values
    return jnp.clip(values, min=-limit, max=limit).astype(kind)


def setup_inputs(seed: int = 0) -> dict:
    arg_keys = jax.random.split(jax.random.key(seed), 6)
    return {
        "tokens": scatter_about(arg_keys[0], (TOKENS, D), 1.0, 6.0, ((0, 8),)),
        "weight_codes": draw_weight_codes(jax.random.fold_in(arg_keys[5], 71), 0),
        "scales": jnp.clip(jnp.exp(math.log(0.0003) - 2.3025852 * jax.random.uniform(arg_keys[2], (D // QB, FF), jnp.float32) ** block_levels(arg_keys[2], (D // QB, FF), ((0, 4), (1, 4)), -0.2, 0.2)), 2.9999999242136255e-05, 0.0003),
        "cotangent": scatter_about(arg_keys[3], (TOKENS, FF), 1.0, 6.0, ((0, 8), (1, 4))),
        "sign_bits": plant(jax.random.randint(arg_keys[4], (FF,), 0, 2), jax.random.fold_in(arg_keys[4], 1), 0, 1).astype(jnp.int32),
    }


def hadamard_table(length):
    indices = jnp.arange(length, dtype=jnp.int32)
    intersection_bits = jnp.bitwise_and(indices[:, None], indices[None, :])
    parity = jnp.zeros((length, length), jnp.int32)
    for bit_pos in range(length.bit_length() - 1):
        parity = parity + jnp.bitwise_and(jnp.right_shift(intersection_bits, bit_pos), 1)
    return (1 - 2 * (parity % 2)).astype(jnp.float32)

def rotate_blocks(matrix, sign_bits, scaling):
    height, width = matrix.shape
    signed = matrix * (2 * sign_bits - 1).astype(jnp.float32)[None, :]
    blocks = signed.reshape(height, width // HB, HB)
    turned = jnp.einsum('rbi,ij->rbj', blocks, hadamard_table(HB), precision=lax.Precision.HIGHEST)
    return turned.reshape(height, width) * scaling

def reference(tokens, weight_codes, scales, cotangent, sign_bits):
    weight = (weight_codes.astype(jnp.float32).reshape(D // QB, QB, FF) * scales[:, None, :]).reshape(D, FF).astype(jnp.bfloat16)
    shard_rows = D // N_FSDP

    def add_shard(totals, position):
        offset = (position * shard_rows).astype(jnp.int32)
        token_part = lax.dynamic_slice_in_dim(tokens, offset, shard_rows, 1)
        weight_part = lax.dynamic_slice_in_dim(weight, offset, shard_rows, 0)
        product = jnp.dot(token_part, weight_part, preferred_element_type=jnp.float32).astype(jnp.bfloat16)
        product = lax.optimization_barrier(product)
        return (totals + product.astype(jnp.float32), None)
    hidden, _ = lax.scan(add_shard, jnp.zeros((TOKENS, FF), jnp.float32), jnp.arange(N_FSDP, dtype=jnp.int32))
    sigmoid_val = jax.nn.sigmoid(hidden)
    activation = (hidden * sigmoid_val).astype(jnp.bfloat16)
    hidden_grad = (cotangent.astype(jnp.float32) * sigmoid_val * (1.0 + hidden * (1.0 - sigmoid_val))).astype(jnp.bfloat16)
    weight_grad = jnp.dot(tokens.T, hidden_grad, preferred_element_type=jnp.float32)
    scaling = 1.0 / jnp.sqrt(jnp.float32(HB) * jnp.float32(TOKENS))
    grad_codes = rotate_blocks(weight_grad, sign_bits, scaling)
    quarter = FF // N_TENSOR

    def add_quarter(totals, position):
        offset = (position * quarter).astype(jnp.int32)
        grad_part = lax.dynamic_slice_in_dim(hidden_grad, offset, quarter, 1)
        weight_part = lax.dynamic_slice_in_dim(weight, offset, quarter, 1)
        product = jnp.dot(grad_part, weight_part.T, preferred_element_type=jnp.float32).astype(jnp.bfloat16)
        product = lax.optimization_barrier(product)
        return (totals + product.astype(jnp.float32), None)
    summed, _ = lax.scan(add_quarter, jnp.zeros((TOKENS, D), jnp.float32), jnp.arange(N_TENSOR, dtype=jnp.int32))
    return (activation, summed.astype(jnp.bfloat16), grad_codes)
```

```python
import functools

import jax
import jax.numpy as jnp
from jax import lax
from jax.experimental import pallas as pl
from jax.experimental.pallas import tpu as pltpu
from jax.sharding import PartitionSpec as P

HB = 128


def hadamard_table(length):
    indices = jnp.arange(length, dtype=jnp.int32)
    intersection_bits = jnp.bitwise_and(indices[:, None], indices[None, :])
    parity = jnp.zeros((length, length), jnp.int32)
    for bit_pos in range(length.bit_length() - 1):
        parity = parity + jnp.bitwise_and(jnp.right_shift(intersection_bits, bit_pos), 1)
    return (1 - 2 * (parity % 2)).astype(jnp.bfloat16)


def grad_kernel(scaling, turned_ref, mine_ref, other_ref, sign_ref, table_ref, out_ref, rotated):
    half, width = mine_ref.shape
    for part, ref in enumerate((mine_ref, other_ref)):
        for block in range(width // HB):
            cols = slice(block * HB, (block + 1) * HB)
            signed = ref[:, cols] * sign_ref[:, cols]
            rotated[part * half:(part + 1) * half, cols] = jnp.dot(
                signed, table_ref[...], preferred_element_type=jnp.float32
            ).astype(jnp.bfloat16)
    out_ref[...] = scaling * jnp.dot(turned_ref[...], rotated[...], preferred_element_type=jnp.float32)


def rotated_grad(turned, mine, other, sign_bits):
    rows, total = turned.shape
    half, width = mine.shape
    tile = next(t for t in (512, 256, HB) if width % t == 0)
    signs = (2 * sign_bits - 1).astype(jnp.bfloat16)[None, :]
    scaling = float(1.0 / (HB * total) ** 0.5)
    column = lambda c: (0, c)
    fixed = lambda c: (0, 0)
    return pl.pallas_call(
        functools.partial(grad_kernel, scaling),
        grid=(width // tile,),
        out_shape=jax.ShapeDtypeStruct((rows, width), jnp.float32),
        in_specs=[
            pl.BlockSpec((rows, total), fixed),
            pl.BlockSpec((half, tile), column),
            pl.BlockSpec((half, tile), column),
            pl.BlockSpec((1, tile), column),
            pl.BlockSpec((HB, HB), fixed),
        ],
        out_specs=pl.BlockSpec((rows, tile), column),
        scratch_shapes=[pltpu.VMEM((total, tile), jnp.bfloat16)],
        compiler_params=pltpu.CompilerParams(vmem_limit_bytes=48 * 1024 * 1024),
        cost_estimate=pl.CostEstimate(
            flops=2 * rows * total * width, bytes_accessed=4 * rows * width + 2 * total * width, transcendentals=0
        ),
        name="rotated_grad",
    )(turned, mine, other, signs, hadamard_table(HB))


def partner(array):
    return lax.ppermute(array, "replica", [(0, 1), (1, 0)])


def shards(tokens, weight_codes, scales, cotangent, sign_bits):
    n_fsdp, n_tensor = lax.axis_size("fsdp"), lax.axis_size("tensor")
    local_tokens = tokens.shape[0]
    shard_rows, hidden_cols = weight_codes.shape
    block_rows = shard_rows // scales.shape[0]
    weight = (
        (
            weight_codes.astype(jnp.float32).reshape(scales.shape[0], block_rows, hidden_cols)
            * scales[:, None, :]
        )
        .reshape(shard_rows, hidden_cols)
        .astype(jnp.bfloat16)
    )
    piece = shard_rows // n_tensor
    own = lax.dynamic_slice_in_dim(
        tokens.reshape(local_tokens, n_fsdp, shard_rows), lax.axis_index("tensor") * piece, piece, 2
    ).reshape(local_tokens, n_fsdp * piece)
    quarter = lax.all_to_all(own, "fsdp", split_axis=1, concat_axis=0, tiled=True)
    columns = lax.all_gather(quarter, "tensor", axis=1, tiled=True)
    half_rows = shard_rows // 2
    replica = lax.axis_index("replica")
    kept = lax.dynamic_slice_in_dim(columns, replica * half_rows, half_rows, 1)
    sent = lax.dynamic_slice_in_dim(columns, (1 - replica) * half_rows, half_rows, 1)
    turned = jnp.concatenate([kept, partner(sent)], axis=0).T
    hidden = lax.psum_scatter(
        jnp.dot(columns, weight, preferred_element_type=jnp.float32).astype(jnp.bfloat16),
        "fsdp",
        scatter_dimension=0,
        tiled=True,
    ).astype(jnp.float32)
    sigmoid_val = jax.nn.sigmoid(hidden)
    activation = (hidden * sigmoid_val).astype(jnp.bfloat16)
    hidden_grad = (
        cotangent.astype(jnp.float32) * sigmoid_val * (1.0 + hidden * (1.0 - sigmoid_val))
    ).astype(jnp.bfloat16)
    arrived = lax.all_gather(hidden_grad, "fsdp", axis=0, tiled=True)
    other = partner(arrived)
    product = lax.dot_general(
        arrived, weight, (((1,), (1,)), ((), ())), preferred_element_type=jnp.float32
    ).astype(jnp.bfloat16)
    if n_fsdp == n_tensor:
        summed = lax.psum_scatter(product, "tensor", scatter_dimension=0, tiled=True)
        swap = [(f * n_tensor + t, t * n_tensor + f) for f in range(n_fsdp) for t in range(n_tensor)]
        input_grad = lax.ppermute(summed, ("fsdp", "tensor"), swap)
    else:
        returned = lax.all_to_all(product, "fsdp", split_axis=0, concat_axis=1, tiled=True)
        input_grad = lax.psum_scatter(returned, "tensor", scatter_dimension=1, tiled=True)
    grad_codes = rotated_grad(turned, arrived, other, sign_bits)
    return (activation, input_grad, grad_codes)


def solution(mesh):
    return jax.shard_map(
        shards,
        mesh=mesh,
        in_specs=(
            P(("fsdp", "replica"), None),
            P("fsdp", "tensor"),
            P("fsdp", "tensor"),
            P(("fsdp", "replica"), "tensor"),
            P("tensor"),
        ),
        out_specs=(
            P(("fsdp", "replica"), "tensor"),
            P(("fsdp", "replica"), "tensor"),
            P(("fsdp", "replica"), "tensor"),
        ),
        check_vma=False,
    )
```

```python
import functools

import jax
import jax.numpy as jnp
from jax import lax
from jax.experimental import pallas as pl
from jax.experimental.pallas import tpu as pltpu
from jax.sharding import PartitionSpec as P

HB = 128


def hadamard_table(length):
    indices = jnp.arange(length, dtype=jnp.int32)
    intersection_bits = jnp.bitwise_and(indices[:, None], indices[None, :])
    parity = jnp.zeros((length, length), jnp.int32)
    for bit_pos in range(length.bit_length() - 1):
        parity = parity + jnp.bitwise_and(jnp.right_shift(intersection_bits, bit_pos), 1)
    return (1 - 2 * (parity % 2)).astype(jnp.bfloat16)


def grad_kernel(scaling, turned_ref, mine_ref, other_ref, sign_ref, table_ref, out_ref, rotated):
    half, width = mine_ref.shape
    for part, ref in enumerate((mine_ref, other_ref)):
        for block in range(width // HB):
            cols = slice(block * HB, (block + 1) * HB)
            signed = ref[:, cols] * sign_ref[:, cols]
            rotated[part * half:(part + 1) * half, cols] = jnp.dot(
                signed, table_ref[...], preferred_element_type=jnp.float32
            ).astype(jnp.bfloat16)
    out_ref[...] = scaling * jnp.dot(turned_ref[...], rotated[...], preferred_element_type=jnp.float32)


def rotated_grad(turned, mine, other, sign_bits):
    rows, total = turned.shape
    half, width = mine.shape
    tile = next(t for t in (512, 256, HB) if width % t == 0)
    signs = (2 * sign_bits - 1).astype(jnp.bfloat16)[None, :]
    scaling = float(1.0 / (HB * total) ** 0.5)
    column = lambda c: (0, c)
    fixed = lambda c: (0, 0)
    return pl.pallas_call(
        functools.partial(grad_kernel, scaling),
        grid=(width // tile,),
        out_shape=jax.ShapeDtypeStruct((rows, width), jnp.float32),
        in_specs=[
            pl.BlockSpec((rows, total), fixed),
            pl.BlockSpec((half, tile), column),
            pl.BlockSpec((half, tile), column),
            pl.BlockSpec((1, tile), column),
            pl.BlockSpec((HB, HB), fixed),
        ],
        out_specs=pl.BlockSpec((rows, tile), column),
        scratch_shapes=[pltpu.VMEM((total, tile), jnp.bfloat16)],
        compiler_params=pltpu.CompilerParams(vmem_limit_bytes=48 * 1024 * 1024),
        cost_estimate=pl.CostEstimate(
            flops=2 * rows * total * width, bytes_accessed=4 * rows * width + 2 * total * width, transcendentals=0
        ),
        name="rotated_grad",
    )(turned, mine, other, signs, hadamard_table(HB))


MESH = pl.DeviceIdType.MESH


def line_kernel(
    n, width, part_ref, cot_ref, act_ref, mine_ref, other_ref,
    sums, from_left, from_right, total,
    sum_sent, left_came, right_came, up_sent, down_sent, came, cross_sent, cross_came,
):
    me = lax.axis_index("fsdp")
    partner_id = 1 - lax.axis_index("replica")
    high = jnp.minimum(me + 1, n - 1)
    low = jnp.maximum(me - 1, 0)
    rows = cot_ref.shape[0]
    blocks = cot_ref.shape[1] // width
    has_low, has_high = me > 0, me < n - 1

    def at(ref, owner, c):
        start = owner * rows if isinstance(owner, int) else pl.multiple_of(owner * rows, rows)
        return ref.at[pl.ds(start, rows), pl.ds(pl.multiple_of(c * width, width), width)]

    def move(source, target, owner, c, send, recv, device):
        return pltpu.make_async_remote_copy(
            src_ref=at(source, owner, c), dst_ref=at(target, owner, c),
            send_sem=send.at[owner, c], recv_sem=recv.at[owner, c],
            device_id=device, device_id_type=MESH,
        )

    def sum_up(d, c):
        return move(sums, from_left, d, c, sum_sent, left_came, {"fsdp": high})

    def sum_down(d, c):
        return move(sums, from_right, d, c, sum_sent, right_came, {"fsdp": low})

    def go_up(s, c):
        return move(mine_ref, mine_ref, s, c, up_sent, came, {"fsdp": high})

    def go_down(s, c):
        return move(mine_ref, mine_ref, s, c, down_sent, came, {"fsdp": low})

    def cross(s, c):
        return move(mine_ref, other_ref, s, c, cross_sent, cross_came, {"replica": partner_id})

    def within(c):
        return jnp.logical_and(c >= 0, c < blocks)

    barrier = pltpu.get_barrier_semaphore()
    pl.semaphore_signal(barrier, inc=1, device_id={"replica": partner_id}, device_id_type=MESH)

    @pl.when(has_low)
    def _():
        pl.semaphore_signal(barrier, inc=1, device_id={"fsdp": low}, device_id_type=MESH)

    @pl.when(has_high)
    def _():
        pl.semaphore_signal(barrier, inc=1, device_id={"fsdp": high}, device_id_type=MESH)

    pl.semaphore_wait(barrier, 1 + jnp.where(has_low, 1, 0) + jnp.where(has_high, 1, 0))

    def reduce_chain(c, first, owners, applies, arrival, send):
        @pl.when(within(c))
        def _():
            for d in owners:
                @pl.when(applies(d))
                def _():
                    @pl.when(first)
                    def _():
                        at(sums, d, c)[...] = at(part_ref, d, c)[...]

                    @pl.when(jnp.logical_not(first))
                    def _():
                        arrival[1](d, c).wait_recv()
                        at(sums, d, c)[...] = (
                            at(part_ref, d, c)[...].astype(jnp.float32)
                            + at(arrival[0], d, c)[...].astype(jnp.float32)
                        ).astype(jnp.bfloat16)
            for d in owners:
                @pl.when(applies(d))
                def _():
                    send(d, c).start()

    def step(i, carry):
        reduce_chain(
            i - me, me == 0, range(n - 1, 0, -1), lambda d: me < d, (from_left, sum_up), sum_up
        )
        reduce_chain(
            i - (n - 1 - me), me == n - 1, range(n - 1), lambda d: me > d, (from_right, sum_down), sum_down
        )
        c = i - (n - 1)

        @pl.when(within(c))
        def _():
            total[...] = at(part_ref, me, c)[...].astype(jnp.float32)

            @pl.when(has_low)
            def _():
                sum_up(me, c).wait_recv()
                total[...] += at(from_left, me, c)[...].astype(jnp.float32)

            @pl.when(has_high)
            def _():
                sum_down(me, c).wait_recv()
                total[...] += at(from_right, me, c)[...].astype(jnp.float32)

            hidden = total[...]
            sig = jax.nn.sigmoid(hidden)
            at(act_ref, 0, c)[...] = (hidden * sig).astype(jnp.bfloat16)
            at(mine_ref, me, c)[...] = (
                at(cot_ref, 0, c)[...].astype(jnp.float32) * sig * (1.0 + hidden * (1.0 - sig))
            ).astype(jnp.bfloat16)

            @pl.when(has_high)
            def _():
                go_up(me, c).start()

            @pl.when(has_low)
            def _():
                go_down(me, c).start()

            cross(me, c).start()

        for k in range(1, n):
            late = i - (n - 1 + k)

            @pl.when(jnp.logical_and(within(late), me - k >= 0))
            def _():
                s = me - k
                go_up(s, late).wait_recv()

                @pl.when(has_high)
                def _():
                    go_up(s, late).start()

                cross(s, late).start()

            @pl.when(jnp.logical_and(within(late), me + k < n))
            def _():
                s = me + k
                go_down(s, late).wait_recv()

                @pl.when(has_low)
                def _():
                    go_down(s, late).start()

                cross(s, late).start()

        return carry

    lax.fori_loop(0, blocks + 2 * (n - 1), step, 0)

    def drain(c, carry):
        for d in range(n):
            @pl.when(me != d)
            def _():
                sum_up(d, c).wait_send()

            @pl.when(jnp.logical_and(has_high, me >= d))
            def _():
                go_up(d, c).wait_send()

            @pl.when(jnp.logical_and(has_low, me <= d))
            def _():
                go_down(d, c).wait_send()

            cross(d, c).wait_send()
            cross(d, c).wait_recv()
        return carry

    lax.fori_loop(0, blocks, drain, 0)


def line_exchange(partial, cotangent, n):
    rows, cols = partial.shape
    width = next(t for t in (512, 256, HB) if cols % t == 0)
    vmem = pl.BlockSpec(memory_space=pltpu.VMEM)
    whole = jax.ShapeDtypeStruct((rows, cols), jnp.bfloat16)
    sems = pltpu.SemaphoreType.DMA((n, cols // width))
    return pl.pallas_call(
        functools.partial(line_kernel, n, width),
        out_shape=(jax.ShapeDtypeStruct(cotangent.shape, jnp.bfloat16), whole, whole),
        in_specs=[vmem, vmem],
        out_specs=(vmem, vmem, vmem),
        scratch_shapes=[pltpu.VMEM((rows, cols), jnp.bfloat16)] * 3
        + [pltpu.VMEM((rows // n, width), jnp.float32)]
        + [sems] * 8,
        compiler_params=pltpu.CompilerParams(
            collective_id=0, has_side_effects=True, vmem_limit_bytes=60 * 1024 * 1024
        ),
        name="line_exchange",
    )(partial, cotangent)


def halve(array, keep, n_tensor, bit):
    lead = lax.dynamic_index_in_dim(array, keep, 0, keepdims=False)
    sent = lax.dynamic_index_in_dim(array, 1 - keep, 0, keepdims=False)
    came = lax.ppermute(sent, "tensor", [(t, t ^ bit) for t in range(n_tensor)])
    return (lead.astype(jnp.float32) + came.astype(jnp.float32)).astype(jnp.bfloat16)


def tensor_reduce(product, n_tensor):
    if n_tensor != 4:
        return lax.psum_scatter(product, "tensor", scatter_dimension=0, tiled=True)
    rows, cols = product.shape
    place = lax.axis_index("tensor")
    chunks = product.reshape(2, 2, rows // 4, cols).swapaxes(0, 1)
    chunks = halve(chunks, place % 2, n_tensor, 1)
    return halve(chunks, place // 2, n_tensor, 2)


def partner(array):
    return lax.ppermute(array, "replica", [(0, 1), (1, 0)])


def shards(tokens, weight_codes, scales, cotangent, sign_bits):
    n_fsdp, n_tensor = lax.axis_size("fsdp"), lax.axis_size("tensor")
    local_tokens = tokens.shape[0]
    shard_rows, hidden_cols = weight_codes.shape
    block_rows = shard_rows // scales.shape[0]
    weight = (
        (
            weight_codes.astype(jnp.float32).reshape(scales.shape[0], block_rows, hidden_cols)
            * scales[:, None, :]
        )
        .reshape(shard_rows, hidden_cols)
        .astype(jnp.bfloat16)
    )
    piece = shard_rows // n_tensor
    own = lax.dynamic_slice_in_dim(
        tokens.reshape(local_tokens, n_fsdp, shard_rows), lax.axis_index("tensor") * piece, piece, 2
    ).reshape(local_tokens, n_fsdp * piece)
    quarter = lax.all_to_all(own, "fsdp", split_axis=1, concat_axis=0, tiled=True)
    columns = lax.all_gather(quarter, "tensor", axis=1, tiled=True)
    half_rows = shard_rows // 2
    replica = lax.axis_index("replica")
    kept = lax.dynamic_slice_in_dim(columns, replica * half_rows, half_rows, 1)
    sent = lax.dynamic_slice_in_dim(columns, (1 - replica) * half_rows, half_rows, 1)
    turned = jnp.concatenate([kept, partner(sent)], axis=0).T
    partial = jnp.dot(columns, weight, preferred_element_type=jnp.float32).astype(jnp.bfloat16)
    if n_fsdp > 1 and 12 * partial.size <= 40 * 1024 * 1024:
        activation, arrived, other = line_exchange(partial, cotangent, n_fsdp)
    else:
        hidden = lax.psum_scatter(partial, "fsdp", scatter_dimension=0, tiled=True).astype(jnp.float32)
        sigmoid_val = jax.nn.sigmoid(hidden)
        activation = (hidden * sigmoid_val).astype(jnp.bfloat16)
        hidden_grad = (
            cotangent.astype(jnp.float32) * sigmoid_val * (1.0 + hidden * (1.0 - sigmoid_val))
        ).astype(jnp.bfloat16)
        arrived = lax.all_gather(hidden_grad, "fsdp", axis=0, tiled=True)
        other = partner(arrived)
    product = lax.dot_general(
        arrived, weight, (((1,), (1,)), ((), ())), preferred_element_type=jnp.float32
    ).astype(jnp.bfloat16)
    if n_fsdp == n_tensor:
        summed = tensor_reduce(product, n_tensor)
        swap = [(f * n_tensor + t, t * n_tensor + f) for f in range(n_fsdp) for t in range(n_tensor)]
        input_grad = lax.ppermute(summed, ("fsdp", "tensor"), swap)
    else:
        returned = lax.all_to_all(product, "fsdp", split_axis=0, concat_axis=1, tiled=True)
        input_grad = lax.psum_scatter(returned, "tensor", scatter_dimension=1, tiled=True)
    grad_codes = rotated_grad(turned, arrived, other, sign_bits)
    return (activation, input_grad, grad_codes)


def solution(mesh):
    return jax.shard_map(
        shards,
        mesh=mesh,
        in_specs=(
            P(("fsdp", "replica"), None),
            P("fsdp", "tensor"),
            P("fsdp", "tensor"),
            P(("fsdp", "replica"), "tensor"),
            P("tensor"),
        ),
        out_specs=(
            P(("fsdp", "replica"), "tensor"),
            P(("fsdp", "replica"), "tensor"),
            P(("fsdp", "replica"), "tensor"),
        ),
        check_vma=False,
    )
```

```python
import functools

import jax
import jax.numpy as jnp
from jax import lax
from jax.experimental import pallas as pl
from jax.experimental.pallas import tpu as pltpu
from jax.sharding import PartitionSpec as P

HB = 128


def hadamard_table(length):
    indices = jnp.arange(length, dtype=jnp.int32)
    intersection_bits = jnp.bitwise_and(indices[:, None], indices[None, :])
    parity = jnp.zeros((length, length), jnp.int32)
    for bit_pos in range(length.bit_length() - 1):
        parity = parity + jnp.bitwise_and(jnp.right_shift(intersection_bits, bit_pos), 1)
    return (1 - 2 * (parity % 2)).astype(jnp.bfloat16)


def grad_kernel(scaling, turned_ref, mine_ref, other_ref, sign_ref, table_ref, out_ref, rotated):
    half, width = mine_ref.shape
    for part, ref in enumerate((mine_ref, other_ref)):
        for block in range(width // HB):
            cols = slice(block * HB, (block + 1) * HB)
            signed = ref[:, cols] * sign_ref[:, cols]
            rotated[part * half:(part + 1) * half, cols] = jnp.dot(
                signed, table_ref[...], preferred_element_type=jnp.float32
            ).astype(jnp.bfloat16)
    out_ref[...] = scaling * jnp.dot(turned_ref[...], rotated[...], preferred_element_type=jnp.float32)


def rotated_grad(turned, mine, other, sign_bits):
    rows, total = turned.shape
    half, width = mine.shape
    tile = next(t for t in (512, 256, HB) if width % t == 0)
    signs = (2 * sign_bits - 1).astype(jnp.bfloat16)[None, :]
    scaling = float(1.0 / (HB * total) ** 0.5)
    column = lambda c: (0, c)
    fixed = lambda c: (0, 0)
    return pl.pallas_call(
        functools.partial(grad_kernel, scaling),
        grid=(width // tile,),
        out_shape=jax.ShapeDtypeStruct((rows, width), jnp.float32),
        in_specs=[
            pl.BlockSpec((rows, total), fixed),
            pl.BlockSpec((half, tile), column),
            pl.BlockSpec((half, tile), column),
            pl.BlockSpec((1, tile), column),
            pl.BlockSpec((HB, HB), fixed),
        ],
        out_specs=pl.BlockSpec((rows, tile), column),
        scratch_shapes=[pltpu.VMEM((total, tile), jnp.bfloat16)],
        compiler_params=pltpu.CompilerParams(vmem_limit_bytes=48 * 1024 * 1024),
        cost_estimate=pl.CostEstimate(
            flops=2 * rows * total * width, bytes_accessed=4 * rows * width + 2 * total * width, transcendentals=0
        ),
        name="rotated_grad",
    )(turned, mine, other, signs, hadamard_table(HB))


MESH = pl.DeviceIdType.MESH


def line_kernel(
    n, width, tokens_ref, weight_hbm, cot_ref, act_ref, mine_ref, other_ref, product_ref, across_ref,
    part_ref, sums, from_left, from_right, total, weight_ref, gathered, fetched, swap_sent, swap_came,
    sum_sent, left_came, right_came, up_sent, down_sent, came, cross_sent, cross_came,
):
    me = lax.axis_index("fsdp")
    partner_id = 1 - lax.axis_index("replica")
    high = jnp.minimum(me + 1, n - 1)
    low = jnp.maximum(me - 1, 0)
    rows = cot_ref.shape[0]
    blocks = cot_ref.shape[1] // width
    has_low, has_high = me > 0, me < n - 1

    def at(ref, owner, c):
        start = owner * rows if isinstance(owner, int) else pl.multiple_of(owner * rows, rows)
        return ref.at[pl.ds(start, rows), pl.ds(pl.multiple_of(c * width, width), width)]

    def move(source, target, owner, c, send, recv, device):
        return pltpu.make_async_remote_copy(
            src_ref=at(source, owner, c), dst_ref=at(target, owner, c),
            send_sem=send.at[owner, c], recv_sem=recv.at[owner, c],
            device_id=device, device_id_type=MESH,
        )

    def sum_up(d, c):
        return move(sums, from_left, d, c, sum_sent, left_came, {"fsdp": high})

    def sum_down(d, c):
        return move(sums, from_right, d, c, sum_sent, right_came, {"fsdp": low})

    def go_up(s, c):
        return move(mine_ref, mine_ref, s, c, up_sent, came, {"fsdp": high})

    def go_down(s, c):
        return move(mine_ref, mine_ref, s, c, down_sent, came, {"fsdp": low})

    def cross(s, c):
        return move(mine_ref, other_ref, s, c, cross_sent, cross_came, {"replica": partner_id})

    def within(c):
        return jnp.logical_and(c >= 0, c < blocks)

    def fetch(c):
        cols = pl.ds(pl.multiple_of(c * width, width), width)
        return pltpu.make_async_copy(weight_hbm.at[:, cols], weight_ref.at[:, cols], fetched.at[c])

    def fetch_all(c, carry):
        fetch(c).start()
        return carry

    lax.fori_loop(0, blocks, fetch_all, 0)

    def project(c):
        fetch(c).wait()
        cols = pl.ds(pl.multiple_of(c * width, width), width)
        part_ref[:, cols] = jnp.dot(
            tokens_ref[...], weight_ref[:, cols], preferred_element_type=jnp.float32
        ).astype(jnp.bfloat16)

    barrier = pltpu.get_barrier_semaphore()
    pl.semaphore_signal(barrier, inc=1, device_id={"replica": partner_id}, device_id_type=MESH)

    @pl.when(has_low)
    def _():
        pl.semaphore_signal(barrier, inc=1, device_id={"fsdp": low}, device_id_type=MESH)

    @pl.when(has_high)
    def _():
        pl.semaphore_signal(barrier, inc=1, device_id={"fsdp": high}, device_id_type=MESH)

    pl.semaphore_wait(barrier, 1 + jnp.where(has_low, 1, 0) + jnp.where(has_high, 1, 0))

    depth = across_ref.shape[1]
    swap = pltpu.make_async_remote_copy(
        src_ref=tokens_ref.at[:, pl.ds(pl.multiple_of(partner_id * depth, depth), depth)],
        dst_ref=across_ref, send_sem=swap_sent, recv_sem=swap_came,
        device_id={"replica": partner_id}, device_id_type=MESH,
    )
    swap.start()
    gathered[...] = jnp.zeros_like(gathered)
    project(0)

    def reduce_chain(c, first, owners, applies, arrival, send):
        @pl.when(within(c))
        def _():
            for d in owners:
                @pl.when(applies(d))
                def _():
                    @pl.when(first)
                    def _():
                        at(sums, d, c)[...] = at(part_ref, d, c)[...]

                    @pl.when(jnp.logical_not(first))
                    def _():
                        arrival[1](d, c).wait_recv()
                        at(sums, d, c)[...] = (
                            at(part_ref, d, c)[...].astype(jnp.float32)
                            + at(arrival[0], d, c)[...].astype(jnp.float32)
                        ).astype(jnp.bfloat16)
            for d in owners:
                @pl.when(applies(d))
                def _():
                    send(d, c).start()

    def step(i, carry):
        reduce_chain(
            i - me, me == 0, range(n - 1, 0, -1), lambda d: me < d, (from_left, sum_up), sum_up
        )
        reduce_chain(
            i - (n - 1 - me), me == n - 1, range(n - 1), lambda d: me > d, (from_right, sum_down), sum_down
        )
        c = i - (n - 1)

        @pl.when(within(c))
        def _():
            total[...] = at(part_ref, me, c)[...].astype(jnp.float32)

            @pl.when(has_low)
            def _():
                sum_up(me, c).wait_recv()
                total[...] += at(from_left, me, c)[...].astype(jnp.float32)

            @pl.when(has_high)
            def _():
                sum_down(me, c).wait_recv()
                total[...] += at(from_right, me, c)[...].astype(jnp.float32)

            hidden = total[...]
            sig = jax.nn.sigmoid(hidden)
            at(act_ref, 0, c)[...] = (hidden * sig).astype(jnp.bfloat16)
            at(mine_ref, me, c)[...] = (
                at(cot_ref, 0, c)[...].astype(jnp.float32) * sig * (1.0 + hidden * (1.0 - sig))
            ).astype(jnp.bfloat16)

            @pl.when(has_high)
            def _():
                go_up(me, c).start()

            @pl.when(has_low)
            def _():
                go_down(me, c).start()

            cross(me, c).start()

        for k in range(1, n):
            late = i - (n - 1 + k)

            @pl.when(jnp.logical_and(within(late), me - k >= 0))
            def _():
                s = me - k
                go_up(s, late).wait_recv()

                @pl.when(has_high)
                def _():
                    go_up(s, late).start()

                cross(s, late).start()

            @pl.when(jnp.logical_and(within(late), me + k < n))
            def _():
                s = me + k
                go_down(s, late).wait_recv()

                @pl.when(has_low)
                def _():
                    go_down(s, late).start()

                cross(s, late).start()

        @pl.when(i + 1 < blocks)
        def _():
            project(i + 1)

        done = i - 2 * (n - 1)

        @pl.when(done >= 0)
        def _():
            cols = pl.ds(pl.multiple_of(done * width, width), width)
            gathered[...] += lax.dot_general(
                mine_ref[:, cols], weight_ref[:, cols], (((1,), (1,)), ((), ())),
                preferred_element_type=jnp.float32,
            )

        return carry

    lax.fori_loop(0, blocks + 2 * (n - 1), step, 0)

    product_ref[...] = gathered[...].astype(jnp.bfloat16)
    swap.wait()

    def drain(c, carry):
        for d in range(n):
            @pl.when(me != d)
            def _():
                sum_up(d, c).wait_send()

            @pl.when(jnp.logical_and(has_high, me >= d))
            def _():
                go_up(d, c).wait_send()

            @pl.when(jnp.logical_and(has_low, me <= d))
            def _():
                go_down(d, c).wait_send()

            cross(d, c).wait_send()
            cross(d, c).wait_recv()
        return carry

    lax.fori_loop(0, blocks, drain, 0)


def line_exchange(columns, weight, cotangent, n):
    rows, depth = columns.shape
    cols = weight.shape[1]
    width = next(t for t in (256, HB) if cols % t == 0)
    vmem = pl.BlockSpec(memory_space=pltpu.VMEM)
    whole = jax.ShapeDtypeStruct((rows, cols), jnp.bfloat16)
    sems = pltpu.SemaphoreType.DMA((n, cols // width))
    return pl.pallas_call(
        functools.partial(line_kernel, n, width),
        out_shape=(
            jax.ShapeDtypeStruct(cotangent.shape, jnp.bfloat16),
            whole,
            whole,
            jax.ShapeDtypeStruct((rows, depth), jnp.bfloat16),
            jax.ShapeDtypeStruct((rows, depth // 2), jnp.bfloat16),
        ),
        in_specs=[vmem, pl.BlockSpec(memory_space=pl.ANY), vmem],
        out_specs=(vmem,) * 5,
        scratch_shapes=[pltpu.VMEM((rows, cols), jnp.bfloat16)] * 4
        + [
            pltpu.VMEM((rows // n, width), jnp.float32),
            pltpu.VMEM(weight.shape, jnp.bfloat16),
            pltpu.VMEM((rows, depth), jnp.float32),
            pltpu.SemaphoreType.DMA((cols // width,)),
            pltpu.SemaphoreType.DMA,
            pltpu.SemaphoreType.DMA,
        ]
        + [sems] * 8,
        compiler_params=pltpu.CompilerParams(
            collective_id=0, has_side_effects=True, vmem_limit_bytes=60 * 1024 * 1024
        ),
        name="line_exchange",
    )(columns, weight, cotangent)


def halve(array, keep, n_tensor, bit):
    lead = lax.dynamic_index_in_dim(array, keep, 0, keepdims=False)
    sent = lax.dynamic_index_in_dim(array, 1 - keep, 0, keepdims=False)
    came = lax.ppermute(sent, "tensor", [(t, t ^ bit) for t in range(n_tensor)])
    return (lead.astype(jnp.float32) + came.astype(jnp.float32)).astype(jnp.bfloat16)


def tensor_reduce(product, n_tensor):
    if n_tensor != 4:
        return lax.psum_scatter(product, "tensor", scatter_dimension=0, tiled=True)
    rows, cols = product.shape
    place = lax.axis_index("tensor")
    chunks = product.reshape(2, 2, rows // 4, cols).swapaxes(0, 1)
    chunks = halve(chunks, place % 2, n_tensor, 1)
    return halve(chunks, place // 2, n_tensor, 2)


def partner(array):
    return lax.ppermute(array, "replica", [(0, 1), (1, 0)])


def shards(tokens, weight_codes, scales, cotangent, sign_bits):
    n_fsdp, n_tensor = lax.axis_size("fsdp"), lax.axis_size("tensor")
    local_tokens = tokens.shape[0]
    shard_rows, hidden_cols = weight_codes.shape
    block_rows = shard_rows // scales.shape[0]
    weight = (
        (
            weight_codes.astype(jnp.float32).reshape(scales.shape[0], block_rows, hidden_cols)
            * scales[:, None, :]
        )
        .reshape(shard_rows, hidden_cols)
        .astype(jnp.bfloat16)
    )
    piece = shard_rows // n_tensor
    own = lax.dynamic_slice_in_dim(
        tokens.reshape(local_tokens, n_fsdp, shard_rows), lax.axis_index("tensor") * piece, piece, 2
    ).reshape(local_tokens, n_fsdp * piece)
    quarter = lax.all_to_all(own, "fsdp", split_axis=1, concat_axis=0, tiled=True)
    columns = lax.all_gather(quarter, "tensor", axis=1, tiled=True)
    half_rows = shard_rows // 2
    replica = lax.axis_index("replica")
    kept = lax.dynamic_slice_in_dim(columns, replica * half_rows, half_rows, 1)
    gathered = n_fsdp * local_tokens
    held = 2 * shard_rows * hidden_cols + 12 * gathered * hidden_cols + 9 * gathered * shard_rows
    if n_fsdp > 1 and held <= 52 * 1024 * 1024:
        activation, arrived, other, product, across = line_exchange(columns, weight, cotangent, n_fsdp)
    else:
        across = partner(lax.dynamic_slice_in_dim(columns, (1 - replica) * half_rows, half_rows, 1))
        hidden = lax.psum_scatter(
            jnp.dot(columns, weight, preferred_element_type=jnp.float32).astype(jnp.bfloat16),
            "fsdp",
            scatter_dimension=0,
            tiled=True,
        ).astype(jnp.float32)
        sigmoid_val = jax.nn.sigmoid(hidden)
        activation = (hidden * sigmoid_val).astype(jnp.bfloat16)
        hidden_grad = (
            cotangent.astype(jnp.float32) * sigmoid_val * (1.0 + hidden * (1.0 - sigmoid_val))
        ).astype(jnp.bfloat16)
        arrived = lax.all_gather(hidden_grad, "fsdp", axis=0, tiled=True)
        other = partner(arrived)
        product = lax.dot_general(
            arrived, weight, (((1,), (1,)), ((), ())), preferred_element_type=jnp.float32
        ).astype(jnp.bfloat16)
    turned = jnp.concatenate([kept, across], axis=0).T
    if n_fsdp == n_tensor:
        summed = tensor_reduce(product, n_tensor)
        swap = [(f * n_tensor + t, t * n_tensor + f) for f in range(n_fsdp) for t in range(n_tensor)]
        input_grad = lax.ppermute(summed, ("fsdp", "tensor"), swap)
    else:
        returned = lax.all_to_all(product, "fsdp", split_axis=0, concat_axis=1, tiled=True)
        input_grad = lax.psum_scatter(returned, "tensor", scatter_dimension=1, tiled=True)
    grad_codes = rotated_grad(turned, arrived, other, sign_bits)
    return (activation, input_grad, grad_codes)


def solution(mesh):
    return jax.shard_map(
        shards,
        mesh=mesh,
        in_specs=(
            P(("fsdp", "replica"), None),
            P("fsdp", "tensor"),
            P("fsdp", "tensor"),
            P(("fsdp", "replica"), "tensor"),
            P("tensor"),
        ),
        out_specs=(
            P(("fsdp", "replica"), "tensor"),
            P(("fsdp", "replica"), "tensor"),
            P(("fsdp", "replica"), "tensor"),
        ),
        check_vma=False,
    )
```

```python
import functools

import jax
import jax.numpy as jnp
from jax import lax
from jax.experimental import pallas as pl
from jax.experimental.pallas import tpu as pltpu
from jax.sharding import PartitionSpec as P

HB = 128


def hadamard_table(length):
    indices = jnp.arange(length, dtype=jnp.int32)
    intersection_bits = jnp.bitwise_and(indices[:, None], indices[None, :])
    parity = jnp.zeros((length, length), jnp.int32)
    for bit_pos in range(length.bit_length() - 1):
        parity = parity + jnp.bitwise_and(jnp.right_shift(intersection_bits, bit_pos), 1)
    return (1 - 2 * (parity % 2)).astype(jnp.bfloat16)


def grad_kernel(scaling, turned_ref, mine_ref, other_ref, sign_ref, table_ref, out_ref, rotated):
    half, width = mine_ref.shape
    for part, ref in enumerate((mine_ref, other_ref)):
        for block in range(width // HB):
            cols = slice(block * HB, (block + 1) * HB)
            signed = ref[:, cols] * sign_ref[:, cols]
            rotated[part * half:(part + 1) * half, cols] = jnp.dot(
                signed, table_ref[...], preferred_element_type=jnp.float32
            ).astype(jnp.bfloat16)
    out_ref[...] = scaling * jnp.dot(turned_ref[...], rotated[...], preferred_element_type=jnp.float32)


def rotated_grad(turned, mine, other, sign_bits):
    rows, total = turned.shape
    half, width = mine.shape
    tile = next(t for t in (512, 256, HB) if width % t == 0)
    signs = (2 * sign_bits - 1).astype(jnp.bfloat16)[None, :]
    scaling = float(1.0 / (HB * total) ** 0.5)
    column = lambda c: (0, c)
    fixed = lambda c: (0, 0)
    return pl.pallas_call(
        functools.partial(grad_kernel, scaling),
        grid=(width // tile,),
        out_shape=jax.ShapeDtypeStruct((rows, width), jnp.float32),
        in_specs=[
            pl.BlockSpec((rows, total), fixed),
            pl.BlockSpec((half, tile), column),
            pl.BlockSpec((half, tile), column),
            pl.BlockSpec((1, tile), column),
            pl.BlockSpec((HB, HB), fixed),
        ],
        out_specs=pl.BlockSpec((rows, tile), column),
        scratch_shapes=[pltpu.VMEM((total, tile), jnp.bfloat16)],
        compiler_params=pltpu.CompilerParams(vmem_limit_bytes=48 * 1024 * 1024),
        cost_estimate=pl.CostEstimate(
            flops=2 * rows * total * width, bytes_accessed=4 * rows * width + 2 * total * width, transcendentals=0
        ),
        name="rotated_grad",
    )(turned, mine, other, signs, hadamard_table(HB))


MESH = pl.DeviceIdType.MESH


def fetch_kernel(
    n, tokens_ref, codes_ref, scales_ref, weight_ref, columns_ref, came,
    out_sent, out_came, mate_sent, mate_came, over_sent, over_came, relay_sent, relay_came,
):
    step, last = pl.program_id(0), pl.num_programs(0) - 1
    me, t = lax.axis_index("fsdp"), lax.axis_index("tensor")
    mate, over = t + 1 - 2 * (t % 2), (t + 2) % 4
    rows = tokens_ref.shape[0]
    depth = tokens_ref.shape[1] // n
    piece = depth // 4

    def spot(s, q):
        return came.at[
            pl.ds(pl.multiple_of(s * rows, rows), rows), pl.ds(pl.multiple_of(q * piece, piece), piece)
        ]

    def send_out(f):
        start = pl.multiple_of(f * depth + t * piece, piece)
        return pltpu.make_async_remote_copy(
            src_ref=tokens_ref.at[:, pl.ds(start, piece)], dst_ref=spot(me, t),
            send_sem=out_sent.at[f], recv_sem=out_came.at[me],
            device_id={"fsdp": f}, device_id_type=MESH,
        )

    def receive_out(s):
        return pltpu.make_async_remote_copy(
            src_ref=spot(s, t), dst_ref=spot(s, t),
            send_sem=out_sent.at[s], recv_sem=out_came.at[s],
            device_id={"fsdp": s}, device_id_type=MESH,
        )

    def pass_on(s, q, sent, arrival, device):
        return pltpu.make_async_remote_copy(
            src_ref=spot(s, q), dst_ref=spot(s, q), send_sem=sent.at[s], recv_sem=arrival.at[s],
            device_id={"tensor": device}, device_id_type=MESH,
        )

    def to_mate(s):
        return pass_on(s, t, mate_sent, mate_came, mate)

    def to_over(s):
        return pass_on(s, t, over_sent, over_came, over)

    def to_relay(s):
        return pass_on(s, over, relay_sent, relay_came, mate)

    @pl.when(step == 0)
    def _():
        barrier = pltpu.get_barrier_semaphore()
        for k in range(1, n):
            pl.semaphore_signal(barrier, inc=1, device_id={"fsdp": (me + k) % n}, device_id_type=MESH)
        pl.semaphore_signal(barrier, inc=1, device_id={"tensor": mate}, device_id_type=MESH)
        pl.semaphore_signal(barrier, inc=1, device_id={"tensor": over}, device_id_type=MESH)
        pl.semaphore_wait(barrier, n + 1)
        for k in range(1, n):
            send_out((me + k) % n).start()
        came[pl.ds(pl.multiple_of(me * rows, rows), rows), :] = tokens_ref[
            :, pl.ds(pl.multiple_of(me * depth, depth), depth)
        ]

    weight_ref[...] = (
        codes_ref[...].astype(jnp.float32) * scales_ref[pl.ds(step, 1), :]
    ).astype(jnp.bfloat16)

    def each(k, act):
        for s in (me - k, me + k):
            @pl.when(jnp.logical_and(s >= 0, s < n))
            def _():
                act(s)

    def forward(s):
        receive_out(s).wait_recv()
        to_mate(s).start()
        to_over(s).start()

    def relay(s):
        to_over(s).wait_recv()
        to_relay(s).start()

    for k in range(1, n):
        @pl.when(step == jnp.minimum(2 + 3 * k, last))
        def _():
            each(k, forward)

    for k in range(1, n):
        @pl.when(step == jnp.minimum(5 + 3 * k, last))
        def _():
            each(k, relay)

    def finish(s):
        to_mate(s).wait_recv()
        to_relay(s).wait_recv()
        send_out(s).wait_send()
        to_mate(s).wait_send()
        to_over(s).wait_send()
        to_relay(s).wait_send()

    @pl.when(step == last)
    def _():
        for k in range(1, n):
            each(k, finish)
        columns_ref[...] = came[...]


def fetch_tokens(tokens, codes, scales, n):
    rows, width = tokens.shape
    shard_rows, cols = codes.shape
    steps = scales.shape[0]
    fixed = lambda i: (0, 0)
    sem = pltpu.SemaphoreType.DMA((n,))
    return pl.pallas_call(
        functools.partial(fetch_kernel, n),
        grid=(steps,),
        out_shape=(
            jax.ShapeDtypeStruct(codes.shape, jnp.bfloat16),
            jax.ShapeDtypeStruct((n * rows, shard_rows), jnp.bfloat16),
        ),
        in_specs=[
            pl.BlockSpec((rows, width), fixed),
            pl.BlockSpec((shard_rows // steps, cols), lambda i: (i, 0)),
            pl.BlockSpec((steps, cols), fixed),
        ],
        out_specs=(
            pl.BlockSpec((shard_rows // steps, cols), lambda i: (i, 0)),
            pl.BlockSpec((n * rows, shard_rows), fixed),
        ),
        scratch_shapes=[pltpu.VMEM((n * rows, shard_rows), jnp.bfloat16)] + [sem] * 8,
        compiler_params=pltpu.CompilerParams(
            collective_id=1, has_side_effects=True, vmem_limit_bytes=48 * 1024 * 1024
        ),
        name="fetch_tokens",
    )(tokens, codes, scales)


def line_kernel(
    n, width, tokens_ref, weight_hbm, cot_ref, act_ref, mine_ref, other_ref, product_ref, across_ref,
    part_ref, sums, from_left, from_right, total, weight_ref, gathered, fetched, swap_sent, swap_came,
    sum_sent, left_came, right_came, up_sent, down_sent, came, cross_sent, cross_came,
):
    me = lax.axis_index("fsdp")
    partner_id = 1 - lax.axis_index("replica")
    high = jnp.minimum(me + 1, n - 1)
    low = jnp.maximum(me - 1, 0)
    rows = cot_ref.shape[0]
    blocks = cot_ref.shape[1] // width
    has_low, has_high = me > 0, me < n - 1

    def at(ref, owner, c):
        start = owner * rows if isinstance(owner, int) else pl.multiple_of(owner * rows, rows)
        return ref.at[pl.ds(start, rows), pl.ds(pl.multiple_of(c * width, width), width)]

    def move(source, target, owner, c, send, recv, device):
        return pltpu.make_async_remote_copy(
            src_ref=at(source, owner, c), dst_ref=at(target, owner, c),
            send_sem=send.at[owner, c], recv_sem=recv.at[owner, c],
            device_id=device, device_id_type=MESH,
        )

    def sum_up(d, c):
        return move(sums, from_left, d, c, sum_sent, left_came, {"fsdp": high})

    def sum_down(d, c):
        return move(sums, from_right, d, c, sum_sent, right_came, {"fsdp": low})

    def go_up(s, c):
        return move(mine_ref, mine_ref, s, c, up_sent, came, {"fsdp": high})

    def go_down(s, c):
        return move(mine_ref, mine_ref, s, c, down_sent, came, {"fsdp": low})

    def cross(s, c):
        return move(mine_ref, other_ref, s, c, cross_sent, cross_came, {"replica": partner_id})

    def within(c):
        return jnp.logical_and(c >= 0, c < blocks)

    def fetch(c):
        cols = pl.ds(pl.multiple_of(c * width, width), width)
        return pltpu.make_async_copy(weight_hbm.at[:, cols], weight_ref.at[:, cols], fetched.at[c])

    def fetch_all(c, carry):
        fetch(c).start()
        return carry

    lax.fori_loop(0, blocks, fetch_all, 0)

    def project(c):
        fetch(c).wait()
        cols = pl.ds(pl.multiple_of(c * width, width), width)
        part_ref[:, cols] = jnp.dot(
            tokens_ref[...], weight_ref[:, cols], preferred_element_type=jnp.float32
        ).astype(jnp.bfloat16)

    barrier = pltpu.get_barrier_semaphore()
    pl.semaphore_signal(barrier, inc=1, device_id={"replica": partner_id}, device_id_type=MESH)

    @pl.when(has_low)
    def _():
        pl.semaphore_signal(barrier, inc=1, device_id={"fsdp": low}, device_id_type=MESH)

    @pl.when(has_high)
    def _():
        pl.semaphore_signal(barrier, inc=1, device_id={"fsdp": high}, device_id_type=MESH)

    pl.semaphore_wait(barrier, 1 + jnp.where(has_low, 1, 0) + jnp.where(has_high, 1, 0))

    depth = across_ref.shape[1]
    swap = pltpu.make_async_remote_copy(
        src_ref=tokens_ref.at[:, pl.ds(pl.multiple_of(partner_id * depth, depth), depth)],
        dst_ref=across_ref, send_sem=swap_sent, recv_sem=swap_came,
        device_id={"replica": partner_id}, device_id_type=MESH,
    )
    swap.start()
    gathered[...] = jnp.zeros_like(gathered)
    project(0)

    def reduce_chain(c, first, owners, applies, arrival, send):
        @pl.when(within(c))
        def _():
            for d in owners:
                @pl.when(applies(d))
                def _():
                    @pl.when(first)
                    def _():
                        at(sums, d, c)[...] = at(part_ref, d, c)[...]

                    @pl.when(jnp.logical_not(first))
                    def _():
                        arrival[1](d, c).wait_recv()
                        at(sums, d, c)[...] = (
                            at(part_ref, d, c)[...].astype(jnp.float32)
                            + at(arrival[0], d, c)[...].astype(jnp.float32)
                        ).astype(jnp.bfloat16)
            for d in owners:
                @pl.when(applies(d))
                def _():
                    send(d, c).start()

    def step(i, carry):
        reduce_chain(
            i - me, me == 0, range(n - 1, 0, -1), lambda d: me < d, (from_left, sum_up), sum_up
        )
        reduce_chain(
            i - (n - 1 - me), me == n - 1, range(n - 1), lambda d: me > d, (from_right, sum_down), sum_down
        )
        c = i - (n - 1)

        @pl.when(within(c))
        def _():
            total[...] = at(part_ref, me, c)[...].astype(jnp.float32)

            @pl.when(has_low)
            def _():
                sum_up(me, c).wait_recv()
                total[...] += at(from_left, me, c)[...].astype(jnp.float32)

            @pl.when(has_high)
            def _():
                sum_down(me, c).wait_recv()
                total[...] += at(from_right, me, c)[...].astype(jnp.float32)

            hidden = total[...]
            sig = jax.nn.sigmoid(hidden)
            at(act_ref, 0, c)[...] = (hidden * sig).astype(jnp.bfloat16)
            at(mine_ref, me, c)[...] = (
                at(cot_ref, 0, c)[...].astype(jnp.float32) * sig * (1.0 + hidden * (1.0 - sig))
            ).astype(jnp.bfloat16)

            @pl.when(has_high)
            def _():
                go_up(me, c).start()

            @pl.when(has_low)
            def _():
                go_down(me, c).start()

            cross(me, c).start()

        for k in range(1, n):
            late = i - (n - 1 + k)

            @pl.when(jnp.logical_and(within(late), me - k >= 0))
            def _():
                s = me - k
                go_up(s, late).wait_recv()

                @pl.when(has_high)
                def _():
                    go_up(s, late).start()

                cross(s, late).start()

            @pl.when(jnp.logical_and(within(late), me + k < n))
            def _():
                s = me + k
                go_down(s, late).wait_recv()

                @pl.when(has_low)
                def _():
                    go_down(s, late).start()

                cross(s, late).start()

        @pl.when(i + 1 < blocks)
        def _():
            project(i + 1)

        done = i - 2 * (n - 1)

        @pl.when(done >= 0)
        def _():
            cols = pl.ds(pl.multiple_of(done * width, width), width)
            gathered[...] += lax.dot_general(
                mine_ref[:, cols], weight_ref[:, cols], (((1,), (1,)), ((), ())),
                preferred_element_type=jnp.float32,
            )

        return carry

    lax.fori_loop(0, blocks + 2 * (n - 1), step, 0)

    product_ref[...] = gathered[...].astype(jnp.bfloat16)
    swap.wait()

    def drain(c, carry):
        for d in range(n):
            @pl.when(me != d)
            def _():
                sum_up(d, c).wait_send()

            @pl.when(jnp.logical_and(has_high, me >= d))
            def _():
                go_up(d, c).wait_send()

            @pl.when(jnp.logical_and(has_low, me <= d))
            def _():
                go_down(d, c).wait_send()

            cross(d, c).wait_send()
            cross(d, c).wait_recv()
        return carry

    lax.fori_loop(0, blocks, drain, 0)


def line_exchange(columns, weight, cotangent, n):
    rows, depth = columns.shape
    cols = weight.shape[1]
    width = next(t for t in (256, HB) if cols % t == 0)
    vmem = pl.BlockSpec(memory_space=pltpu.VMEM)
    whole = jax.ShapeDtypeStruct((rows, cols), jnp.bfloat16)
    sems = pltpu.SemaphoreType.DMA((n, cols // width))
    return pl.pallas_call(
        functools.partial(line_kernel, n, width),
        out_shape=(
            jax.ShapeDtypeStruct(cotangent.shape, jnp.bfloat16),
            whole,
            whole,
            jax.ShapeDtypeStruct((rows, depth), jnp.bfloat16),
            jax.ShapeDtypeStruct((rows, depth // 2), jnp.bfloat16),
        ),
        in_specs=[vmem, pl.BlockSpec(memory_space=pl.ANY), vmem],
        out_specs=(vmem,) * 5,
        scratch_shapes=[pltpu.VMEM((rows, cols), jnp.bfloat16)] * 4
        + [
            pltpu.VMEM((rows // n, width), jnp.float32),
            pltpu.VMEM(weight.shape, jnp.bfloat16),
            pltpu.VMEM((rows, depth), jnp.float32),
            pltpu.SemaphoreType.DMA((cols // width,)),
            pltpu.SemaphoreType.DMA,
            pltpu.SemaphoreType.DMA,
        ]
        + [sems] * 8,
        compiler_params=pltpu.CompilerParams(
            collective_id=0, has_side_effects=True, vmem_limit_bytes=60 * 1024 * 1024
        ),
        name="line_exchange",
    )(columns, weight, cotangent)


def halve(array, keep, n_tensor, bit):
    lead = lax.dynamic_index_in_dim(array, keep, 0, keepdims=False)
    sent = lax.dynamic_index_in_dim(array, 1 - keep, 0, keepdims=False)
    came = lax.ppermute(sent, "tensor", [(t, t ^ bit) for t in range(n_tensor)])
    return (lead.astype(jnp.float32) + came.astype(jnp.float32)).astype(jnp.bfloat16)


def tensor_reduce(product, n_tensor):
    if n_tensor != 4:
        return lax.psum_scatter(product, "tensor", scatter_dimension=0, tiled=True)
    rows, cols = product.shape
    place = lax.axis_index("tensor")
    chunks = product.reshape(2, 2, rows // 4, cols).swapaxes(0, 1)
    chunks = halve(chunks, place % 2, n_tensor, 1)
    return halve(chunks, place // 2, n_tensor, 2)


def partner(array):
    return lax.ppermute(array, "replica", [(0, 1), (1, 0)])


def shards(tokens, weight_codes, scales, cotangent, sign_bits):
    n_fsdp, n_tensor = lax.axis_size("fsdp"), lax.axis_size("tensor")
    local_tokens = tokens.shape[0]
    shard_rows, hidden_cols = weight_codes.shape
    block_rows = shard_rows // scales.shape[0]
    if n_tensor == 4 and 1 < n_fsdp <= 4:
        weight, columns = fetch_tokens(tokens, weight_codes, scales, n_fsdp)
    else:
        weight = (
            (
                weight_codes.astype(jnp.float32).reshape(scales.shape[0], block_rows, hidden_cols)
                * scales[:, None, :]
            )
            .reshape(shard_rows, hidden_cols)
            .astype(jnp.bfloat16)
        )
        piece = shard_rows // n_tensor
        own = lax.dynamic_slice_in_dim(
            tokens.reshape(local_tokens, n_fsdp, shard_rows), lax.axis_index("tensor") * piece, piece, 2
        ).reshape(local_tokens, n_fsdp * piece)
        quarter = lax.all_to_all(own, "fsdp", split_axis=1, concat_axis=0, tiled=True)
        columns = lax.all_gather(quarter, "tensor", axis=1, tiled=True)
    half_rows = shard_rows // 2
    replica = lax.axis_index("replica")
    kept = lax.dynamic_slice_in_dim(columns, replica * half_rows, half_rows, 1)
    gathered = n_fsdp * local_tokens
    held = 2 * shard_rows * hidden_cols + 12 * gathered * hidden_cols + 9 * gathered * shard_rows
    if n_fsdp > 1 and held <= 52 * 1024 * 1024:
        activation, arrived, other, product, across = line_exchange(columns, weight, cotangent, n_fsdp)
    else:
        across = partner(lax.dynamic_slice_in_dim(columns, (1 - replica) * half_rows, half_rows, 1))
        hidden = lax.psum_scatter(
            jnp.dot(columns, weight, preferred_element_type=jnp.float32).astype(jnp.bfloat16),
            "fsdp",
            scatter_dimension=0,
            tiled=True,
        ).astype(jnp.float32)
        sigmoid_val = jax.nn.sigmoid(hidden)
        activation = (hidden * sigmoid_val).astype(jnp.bfloat16)
        hidden_grad = (
            cotangent.astype(jnp.float32) * sigmoid_val * (1.0 + hidden * (1.0 - sigmoid_val))
        ).astype(jnp.bfloat16)
        arrived = lax.all_gather(hidden_grad, "fsdp", axis=0, tiled=True)
        other = partner(arrived)
        product = lax.dot_general(
            arrived, weight, (((1,), (1,)), ((), ())), preferred_element_type=jnp.float32
        ).astype(jnp.bfloat16)
    turned = jnp.concatenate([kept, across], axis=0).T
    if n_fsdp == n_tensor:
        summed = tensor_reduce(product, n_tensor)
        swap = [(f * n_tensor + t, t * n_tensor + f) for f in range(n_fsdp) for t in range(n_tensor)]
        input_grad = lax.ppermute(summed, ("fsdp", "tensor"), swap)
    else:
        returned = lax.all_to_all(product, "fsdp", split_axis=0, concat_axis=1, tiled=True)
        input_grad = lax.psum_scatter(returned, "tensor", scatter_dimension=1, tiled=True)
    grad_codes = rotated_grad(turned, arrived, other, sign_bits)
    return (activation, input_grad, grad_codes)


def solution(mesh):
    return jax.shard_map(
        shards,
        mesh=mesh,
        in_specs=(
            P(("fsdp", "replica"), None),
            P("fsdp", "tensor"),
            P("fsdp", "tensor"),
            P(("fsdp", "replica"), "tensor"),
            P("tensor"),
        ),
        out_specs=(
            P(("fsdp", "replica"), "tensor"),
            P(("fsdp", "replica"), "tensor"),
            P(("fsdp", "replica"), "tensor"),
        ),
        check_vma=False,
    )
```

```python
import functools

import jax
import jax.numpy as jnp
from jax import lax
from jax.experimental import pallas as pl
from jax.experimental.pallas import tpu as pltpu
from jax.sharding import PartitionSpec as P

HB = 128


def hadamard_table(length):
    indices = jnp.arange(length, dtype=jnp.int32)
    intersection_bits = jnp.bitwise_and(indices[:, None], indices[None, :])
    parity = jnp.zeros((length, length), jnp.int32)
    for bit_pos in range(length.bit_length() - 1):
        parity = parity + jnp.bitwise_and(jnp.right_shift(intersection_bits, bit_pos), 1)
    return (1 - 2 * (parity % 2)).astype(jnp.bfloat16)


def grad_kernel(scaling, turned_ref, mine_ref, other_ref, sign_ref, table_ref, out_ref, rotated):
    half, width = mine_ref.shape
    for part, ref in enumerate((mine_ref, other_ref)):
        for block in range(width // HB):
            cols = slice(block * HB, (block + 1) * HB)
            signed = ref[:, cols] * sign_ref[:, cols]
            rotated[part * half:(part + 1) * half, cols] = jnp.dot(
                signed, table_ref[...], preferred_element_type=jnp.float32
            ).astype(jnp.bfloat16)
    out_ref[...] = scaling * jnp.dot(turned_ref[...], rotated[...], preferred_element_type=jnp.float32)


def rotated_grad(turned, mine, other, sign_bits):
    rows, total = turned.shape
    half, width = mine.shape
    tile = next(t for t in (512, 256, HB) if width % t == 0)
    signs = (2 * sign_bits - 1).astype(jnp.bfloat16)[None, :]
    scaling = float(1.0 / (HB * total) ** 0.5)
    column = lambda c: (0, c)
    fixed = lambda c: (0, 0)
    return pl.pallas_call(
        functools.partial(grad_kernel, scaling),
        grid=(width // tile,),
        out_shape=jax.ShapeDtypeStruct((rows, width), jnp.float32),
        in_specs=[
            pl.BlockSpec((rows, total), fixed),
            pl.BlockSpec((half, tile), column),
            pl.BlockSpec((half, tile), column),
            pl.BlockSpec((1, tile), column),
            pl.BlockSpec((HB, HB), fixed),
        ],
        out_specs=pl.BlockSpec((rows, tile), column),
        scratch_shapes=[pltpu.VMEM((total, tile), jnp.bfloat16)],
        compiler_params=pltpu.CompilerParams(vmem_limit_bytes=48 * 1024 * 1024),
        cost_estimate=pl.CostEstimate(
            flops=2 * rows * total * width, bytes_accessed=4 * rows * width + 2 * total * width, transcendentals=0
        ),
        name="rotated_grad",
    )(turned, mine, other, signs, hadamard_table(HB))


MESH = pl.DeviceIdType.MESH


def fetch_kernel(
    n, tokens_ref, codes_ref, scales_ref, weight_ref, columns_ref, came,
    out_sent, out_came, mate_sent, mate_came, over_sent, over_came, relay_sent, relay_came,
):
    step, last = pl.program_id(0), pl.num_programs(0) - 1
    me, t = lax.axis_index("fsdp"), lax.axis_index("tensor")
    mate, over = t + 1 - 2 * (t % 2), (t + 2) % 4
    rows = tokens_ref.shape[0]
    depth = tokens_ref.shape[1] // n
    piece = depth // 4

    def spot(s, q):
        return came.at[
            pl.ds(pl.multiple_of(s * rows, rows), rows), pl.ds(pl.multiple_of(q * piece, piece), piece)
        ]

    def send_out(f):
        start = pl.multiple_of(f * depth + t * piece, piece)
        return pltpu.make_async_remote_copy(
            src_ref=tokens_ref.at[:, pl.ds(start, piece)], dst_ref=spot(me, t),
            send_sem=out_sent.at[f], recv_sem=out_came.at[me],
            device_id={"fsdp": f}, device_id_type=MESH,
        )

    def receive_out(s):
        return pltpu.make_async_remote_copy(
            src_ref=spot(s, t), dst_ref=spot(s, t),
            send_sem=out_sent.at[s], recv_sem=out_came.at[s],
            device_id={"fsdp": s}, device_id_type=MESH,
        )

    def pass_on(s, q, sent, arrival, device):
        return pltpu.make_async_remote_copy(
            src_ref=spot(s, q), dst_ref=spot(s, q), send_sem=sent.at[s], recv_sem=arrival.at[s],
            device_id={"tensor": device}, device_id_type=MESH,
        )

    def to_mate(s):
        return pass_on(s, t, mate_sent, mate_came, mate)

    def to_over(s):
        return pass_on(s, t, over_sent, over_came, over)

    def to_relay(s):
        return pass_on(s, over, relay_sent, relay_came, mate)

    @pl.when(step == 0)
    def _():
        barrier = pltpu.get_barrier_semaphore()
        for k in range(1, n):
            pl.semaphore_signal(barrier, inc=1, device_id={"fsdp": (me + k) % n}, device_id_type=MESH)
        pl.semaphore_signal(barrier, inc=1, device_id={"tensor": mate}, device_id_type=MESH)
        pl.semaphore_signal(barrier, inc=1, device_id={"tensor": over}, device_id_type=MESH)
        pl.semaphore_wait(barrier, n + 1)
        for k in range(1, n):
            send_out((me + k) % n).start()
        came[pl.ds(pl.multiple_of(me * rows, rows), rows), :] = tokens_ref[
            :, pl.ds(pl.multiple_of(me * depth, depth), depth)
        ]

    weight_ref[...] = (
        codes_ref[...].astype(jnp.float32) * scales_ref[pl.ds(step, 1), :]
    ).astype(jnp.bfloat16)

    def each(k, act):
        for s in (me - k, me + k):
            @pl.when(jnp.logical_and(s >= 0, s < n))
            def _():
                act(s)

    def forward(s):
        receive_out(s).wait_recv()
        to_mate(s).start()
        to_over(s).start()

    def relay(s):
        to_over(s).wait_recv()
        to_relay(s).start()

    for k in range(1, n):
        @pl.when(step == jnp.minimum(2 + 3 * k, last))
        def _():
            each(k, forward)

    for k in range(1, n):
        @pl.when(step == jnp.minimum(5 + 3 * k, last))
        def _():
            each(k, relay)

    def finish(s):
        to_mate(s).wait_recv()
        to_relay(s).wait_recv()
        send_out(s).wait_send()
        to_mate(s).wait_send()
        to_over(s).wait_send()
        to_relay(s).wait_send()

    @pl.when(step == last)
    def _():
        for k in range(1, n):
            each(k, finish)
        columns_ref[...] = came[...]


def fetch_tokens(tokens, codes, scales, n):
    rows, width = tokens.shape
    shard_rows, cols = codes.shape
    steps = scales.shape[0]
    fixed = lambda i: (0, 0)
    sem = pltpu.SemaphoreType.DMA((n,))
    return pl.pallas_call(
        functools.partial(fetch_kernel, n),
        grid=(steps,),
        out_shape=(
            jax.ShapeDtypeStruct(codes.shape, jnp.bfloat16),
            jax.ShapeDtypeStruct((n * rows, shard_rows), jnp.bfloat16),
        ),
        in_specs=[
            pl.BlockSpec((rows, width), fixed),
            pl.BlockSpec((shard_rows // steps, cols), lambda i: (i, 0)),
            pl.BlockSpec((steps, cols), fixed),
        ],
        out_specs=(
            pl.BlockSpec((shard_rows // steps, cols), lambda i: (i, 0)),
            pl.BlockSpec((n * rows, shard_rows), fixed),
        ),
        scratch_shapes=[pltpu.VMEM((n * rows, shard_rows), jnp.bfloat16)] + [sem] * 8,
        compiler_params=pltpu.CompilerParams(
            collective_id=1, has_side_effects=True, vmem_limit_bytes=48 * 1024 * 1024
        ),
        name="fetch_tokens",
    )(tokens, codes, scales)


def line_kernel(
    n, width, tokens_ref, weight_hbm, cot_ref, act_ref, mine_ref, other_ref, product_ref, across_ref,
    part_ref, sums, from_left, from_right, total, weight_ref, gathered, fetched, swap_sent, swap_came, pair_sent, pair_came,
    sum_sent, left_came, right_came, up_sent, down_sent, came, cross_sent, cross_came,
):
    me = lax.axis_index("fsdp")
    partner_id = 1 - lax.axis_index("replica")
    mate = lax.axis_index("tensor") + 1 - 2 * (lax.axis_index("tensor") % 2)
    high = jnp.minimum(me + 1, n - 1)
    low = jnp.maximum(me - 1, 0)
    rows = cot_ref.shape[0]
    blocks = cot_ref.shape[1] // width
    has_low, has_high = me > 0, me < n - 1

    def at(ref, owner, c):
        start = owner * rows if isinstance(owner, int) else pl.multiple_of(owner * rows, rows)
        return ref.at[pl.ds(start, rows), pl.ds(pl.multiple_of(c * width, width), width)]

    def move(source, target, owner, c, send, recv, device):
        return pltpu.make_async_remote_copy(
            src_ref=at(source, owner, c), dst_ref=at(target, owner, c),
            send_sem=send.at[owner, c], recv_sem=recv.at[owner, c],
            device_id=device, device_id_type=MESH,
        )

    def sum_up(d, c):
        return move(sums, from_left, d, c, sum_sent, left_came, {"fsdp": high})

    def sum_down(d, c):
        return move(sums, from_right, d, c, sum_sent, right_came, {"fsdp": low})

    def go_up(s, c):
        return move(mine_ref, mine_ref, s, c, up_sent, came, {"fsdp": high})

    def go_down(s, c):
        return move(mine_ref, mine_ref, s, c, down_sent, came, {"fsdp": low})

    def cross(s, c):
        return move(mine_ref, other_ref, s, c, cross_sent, cross_came, {"replica": partner_id})

    def within(c):
        return jnp.logical_and(c >= 0, c < blocks)

    def fetch(c):
        cols = pl.ds(pl.multiple_of(c * width, width), width)
        return pltpu.make_async_copy(weight_hbm.at[:, cols], weight_ref.at[:, cols], fetched.at[c])

    def fetch_all(c, carry):
        fetch(c).start()
        return carry

    lax.fori_loop(0, blocks, fetch_all, 0)

    def project(c):
        fetch(c).wait()
        cols = pl.ds(pl.multiple_of(c * width, width), width)
        part_ref[:, cols] = jnp.dot(
            tokens_ref[...], weight_ref[:, cols], preferred_element_type=jnp.float32
        ).astype(jnp.bfloat16)

    barrier = pltpu.get_barrier_semaphore()
    pl.semaphore_signal(barrier, inc=1, device_id={"replica": partner_id}, device_id_type=MESH)
    pl.semaphore_signal(barrier, inc=1, device_id={"tensor": mate}, device_id_type=MESH)

    @pl.when(has_low)
    def _():
        pl.semaphore_signal(barrier, inc=1, device_id={"fsdp": low}, device_id_type=MESH)

    @pl.when(has_high)
    def _():
        pl.semaphore_signal(barrier, inc=1, device_id={"fsdp": high}, device_id_type=MESH)

    pl.semaphore_wait(barrier, 2 + jnp.where(has_low, 1, 0) + jnp.where(has_high, 1, 0))

    depth = across_ref.shape[1]
    small = depth // 2
    lane = lax.axis_index("tensor") % 2
    share = across_ref.at[:, pl.ds(pl.multiple_of(lane * small, small), small)]
    start = pl.multiple_of(partner_id * depth + lane * small, small)
    swap = pltpu.make_async_remote_copy(
        src_ref=tokens_ref.at[:, pl.ds(start, small)],
        dst_ref=share, send_sem=swap_sent, recv_sem=swap_came,
        device_id={"replica": partner_id}, device_id_type=MESH,
    )
    pair = pltpu.make_async_remote_copy(
        src_ref=share, dst_ref=share, send_sem=pair_sent, recv_sem=pair_came,
        device_id={"tensor": mate}, device_id_type=MESH,
    )
    swap.start()
    gathered[...] = jnp.zeros_like(gathered)
    project(0)

    def reduce_chain(c, first, owners, applies, arrival, send):
        @pl.when(within(c))
        def _():
            for d in owners:
                @pl.when(applies(d))
                def _():
                    @pl.when(first)
                    def _():
                        at(sums, d, c)[...] = at(part_ref, d, c)[...]

                    @pl.when(jnp.logical_not(first))
                    def _():
                        arrival[1](d, c).wait_recv()
                        at(sums, d, c)[...] = (
                            at(part_ref, d, c)[...].astype(jnp.float32)
                            + at(arrival[0], d, c)[...].astype(jnp.float32)
                        ).astype(jnp.bfloat16)
            for d in owners:
                @pl.when(applies(d))
                def _():
                    send(d, c).start()

    def step(i, carry):
        reduce_chain(
            i - me, me == 0, range(n - 1, 0, -1), lambda d: me < d, (from_left, sum_up), sum_up
        )
        reduce_chain(
            i - (n - 1 - me), me == n - 1, range(n - 1), lambda d: me > d, (from_right, sum_down), sum_down
        )
        c = i - (n - 1)

        @pl.when(within(c))
        def _():
            total[...] = at(part_ref, me, c)[...].astype(jnp.float32)

            @pl.when(has_low)
            def _():
                sum_up(me, c).wait_recv()
                total[...] += at(from_left, me, c)[...].astype(jnp.float32)

            @pl.when(has_high)
            def _():
                sum_down(me, c).wait_recv()
                total[...] += at(from_right, me, c)[...].astype(jnp.float32)

            hidden = total[...]
            sig = jax.nn.sigmoid(hidden)
            at(act_ref, 0, c)[...] = (hidden * sig).astype(jnp.bfloat16)
            at(mine_ref, me, c)[...] = (
                at(cot_ref, 0, c)[...].astype(jnp.float32) * sig * (1.0 + hidden * (1.0 - sig))
            ).astype(jnp.bfloat16)

            @pl.when(has_high)
            def _():
                go_up(me, c).start()

            @pl.when(has_low)
            def _():
                go_down(me, c).start()

            cross(me, c).start()

        for k in range(1, n):
            late = i - (n - 1 + k)

            @pl.when(jnp.logical_and(within(late), me - k >= 0))
            def _():
                s = me - k
                go_up(s, late).wait_recv()

                @pl.when(has_high)
                def _():
                    go_up(s, late).start()

                cross(s, late).start()

            @pl.when(jnp.logical_and(within(late), me + k < n))
            def _():
                s = me + k
                go_down(s, late).wait_recv()

                @pl.when(has_low)
                def _():
                    go_down(s, late).start()

                cross(s, late).start()

        @pl.when(i == blocks - 1)
        def _():
            swap.wait()
            pair.start()

        @pl.when(i + 1 < blocks)
        def _():
            project(i + 1)

        done = i - 2 * (n - 1)

        @pl.when(done >= 0)
        def _():
            cols = pl.ds(pl.multiple_of(done * width, width), width)
            gathered[...] += lax.dot_general(
                mine_ref[:, cols], weight_ref[:, cols], (((1,), (1,)), ((), ())),
                preferred_element_type=jnp.float32,
            )

        return carry

    lax.fori_loop(0, blocks + 2 * (n - 1), step, 0)

    product_ref[...] = gathered[...].astype(jnp.bfloat16)
    pair.wait()

    def drain(c, carry):
        for d in range(n):
            @pl.when(me != d)
            def _():
                sum_up(d, c).wait_send()

            @pl.when(jnp.logical_and(has_high, me >= d))
            def _():
                go_up(d, c).wait_send()

            @pl.when(jnp.logical_and(has_low, me <= d))
            def _():
                go_down(d, c).wait_send()

            cross(d, c).wait_send()
            cross(d, c).wait_recv()
        return carry

    lax.fori_loop(0, blocks, drain, 0)


def line_exchange(columns, weight, cotangent, n):
    rows, depth = columns.shape
    cols = weight.shape[1]
    width = next(t for t in (256, HB) if cols % t == 0)
    vmem = pl.BlockSpec(memory_space=pltpu.VMEM)
    whole = jax.ShapeDtypeStruct((rows, cols), jnp.bfloat16)
    sems = pltpu.SemaphoreType.DMA((n, cols // width))
    return pl.pallas_call(
        functools.partial(line_kernel, n, width),
        out_shape=(
            jax.ShapeDtypeStruct(cotangent.shape, jnp.bfloat16),
            whole,
            whole,
            jax.ShapeDtypeStruct((rows, depth), jnp.bfloat16),
            jax.ShapeDtypeStruct((rows, depth // 2), jnp.bfloat16),
        ),
        in_specs=[vmem, pl.BlockSpec(memory_space=pl.ANY), vmem],
        out_specs=(vmem,) * 5,
        scratch_shapes=[pltpu.VMEM((rows, cols), jnp.bfloat16)] * 4
        + [
            pltpu.VMEM((rows // n, width), jnp.float32),
            pltpu.VMEM(weight.shape, jnp.bfloat16),
            pltpu.VMEM((rows, depth), jnp.float32),
            pltpu.SemaphoreType.DMA((cols // width,)),
            pltpu.SemaphoreType.DMA,
            pltpu.SemaphoreType.DMA,
            pltpu.SemaphoreType.DMA,
            pltpu.SemaphoreType.DMA,
        ]
        + [sems] * 8,
        compiler_params=pltpu.CompilerParams(
            collective_id=0, has_side_effects=True, vmem_limit_bytes=60 * 1024 * 1024
        ),
        name="line_exchange",
    )(columns, weight, cotangent)


def halve(array, keep, n_tensor, bit):
    lead = lax.dynamic_index_in_dim(array, keep, 0, keepdims=False)
    sent = lax.dynamic_index_in_dim(array, 1 - keep, 0, keepdims=False)
    came = lax.ppermute(sent, "tensor", [(t, t ^ bit) for t in range(n_tensor)])
    return (lead.astype(jnp.float32) + came.astype(jnp.float32)).astype(jnp.bfloat16)


def tensor_reduce(product, n_tensor):
    if n_tensor != 4:
        return lax.psum_scatter(product, "tensor", scatter_dimension=0, tiled=True)
    rows, cols = product.shape
    place = lax.axis_index("tensor")
    chunks = product.reshape(2, 2, rows // 4, cols).swapaxes(0, 1)
    chunks = halve(chunks, place % 2, n_tensor, 1)
    return halve(chunks, place // 2, n_tensor, 2)


def partner(array):
    return lax.ppermute(array, "replica", [(0, 1), (1, 0)])


def shards(tokens, weight_codes, scales, cotangent, sign_bits):
    n_fsdp, n_tensor = lax.axis_size("fsdp"), lax.axis_size("tensor")
    local_tokens = tokens.shape[0]
    shard_rows, hidden_cols = weight_codes.shape
    block_rows = shard_rows // scales.shape[0]
    if n_tensor == 4 and 1 < n_fsdp <= 4:
        weight, columns = fetch_tokens(tokens, weight_codes, scales, n_fsdp)
    else:
        weight = (
            (
                weight_codes.astype(jnp.float32).reshape(scales.shape[0], block_rows, hidden_cols)
                * scales[:, None, :]
            )
            .reshape(shard_rows, hidden_cols)
            .astype(jnp.bfloat16)
        )
        piece = shard_rows // n_tensor
        own = lax.dynamic_slice_in_dim(
            tokens.reshape(local_tokens, n_fsdp, shard_rows), lax.axis_index("tensor") * piece, piece, 2
        ).reshape(local_tokens, n_fsdp * piece)
        quarter = lax.all_to_all(own, "fsdp", split_axis=1, concat_axis=0, tiled=True)
        columns = lax.all_gather(quarter, "tensor", axis=1, tiled=True)
    half_rows = shard_rows // 2
    replica = lax.axis_index("replica")
    kept = lax.dynamic_slice_in_dim(columns, replica * half_rows, half_rows, 1)
    gathered = n_fsdp * local_tokens
    held = 2 * shard_rows * hidden_cols + 12 * gathered * hidden_cols + 9 * gathered * shard_rows
    if n_fsdp > 1 and n_tensor % 2 == 0 and held <= 52 * 1024 * 1024:
        activation, arrived, other, product, across = line_exchange(columns, weight, cotangent, n_fsdp)
    else:
        across = partner(lax.dynamic_slice_in_dim(columns, (1 - replica) * half_rows, half_rows, 1))
        hidden = lax.psum_scatter(
            jnp.dot(columns, weight, preferred_element_type=jnp.float32).astype(jnp.bfloat16),
            "fsdp",
            scatter_dimension=0,
            tiled=True,
        ).astype(jnp.float32)
        sigmoid_val = jax.nn.sigmoid(hidden)
        activation = (hidden * sigmoid_val).astype(jnp.bfloat16)
        hidden_grad = (
            cotangent.astype(jnp.float32) * sigmoid_val * (1.0 + hidden * (1.0 - sigmoid_val))
        ).astype(jnp.bfloat16)
        arrived = lax.all_gather(hidden_grad, "fsdp", axis=0, tiled=True)
        other = partner(arrived)
        product = lax.dot_general(
            arrived, weight, (((1,), (1,)), ((), ())), preferred_element_type=jnp.float32
        ).astype(jnp.bfloat16)
    turned = jnp.concatenate([kept, across], axis=0).T
    if n_fsdp == n_tensor:
        summed = tensor_reduce(product, n_tensor)
        swap = [(f * n_tensor + t, t * n_tensor + f) for f in range(n_fsdp) for t in range(n_tensor)]
        input_grad = lax.ppermute(summed, ("fsdp", "tensor"), swap)
    else:
        returned = lax.all_to_all(product, "fsdp", split_axis=0, concat_axis=1, tiled=True)
        input_grad = lax.psum_scatter(returned, "tensor", scatter_dimension=1, tiled=True)
    grad_codes = rotated_grad(turned, arrived, other, sign_bits)
    return (activation, input_grad, grad_codes)


def solution(mesh):
    return jax.shard_map(
        shards,
        mesh=mesh,
        in_specs=(
            P(("fsdp", "replica"), None),
            P("fsdp", "tensor"),
            P("fsdp", "tensor"),
            P(("fsdp", "replica"), "tensor"),
            P("tensor"),
        ),
        out_specs=(
            P(("fsdp", "replica"), "tensor"),
            P(("fsdp", "replica"), "tensor"),
            P(("fsdp", "replica"), "tensor"),
        ),
        check_vma=False,
    )
```
